32 devices in a mesh: grp: 2 (over y), tm: 8 (over z, x), row: 2 (over core).
Axes of the slice: x: 2, y: 2, z: 4, core: 2. Of those that a mesh axis runs over, the one named last changes fastest.
Arguments:
- queries: bfloat16 [4096, 768], P(('grp', 'tm', 'row')), parts along dimension 0, may hold values from -5 to 5
- keys: bfloat16 [4096, 768], P(('grp', 'tm', 'row')), parts along dimension 0, may hold values from -5 to 5
- values: bfloat16 [4096, 768], P(('grp', 'tm', 'row')), parts along dimension 0, may hold values from -6 to 6
- d_out: bfloat16 [4096, 768], P(('grp', 'tm', 'row')), parts along dimension 0, may hold values from -6 to 6
- action_table: bfloat16 [8, 768], replicated, may hold values from -5 to 5
- actions: int32 [16], P(('grp', 'tm')), parts along dimension 0, may hold values from 0 to 7
- temporal_list: int32 [32, 2], P(('grp', 'tm', 'row')), parts along dimension 0, may hold values from 1 to 3, as said below
Outputs:
- attended: bfloat16 [4096, 768], P(('grp', 'tm', 'row')), parts along dimension 0
- grad_queries: bfloat16 [4096, 768], P(('grp', 'tm', 'row')), parts along dimension 0
- grad_keys: bfloat16 [4096, 768], P(('grp', 'tm', 'row')), parts along dimension 0
- grad_values: bfloat16 [4096, 768], P(('grp', 'tm', 'row')), parts along dimension 0
- grad_table: float32 [16, 768], P('grp'), parts along dimension 0
The draws below stay inside these ranges and needn't reach their ends.
There are 2 independent parts, one for each index of `grp`. The reference program is written for one: setup_inputs(seed, part) draws one part's arguments, and reference() takes and returns one part's arrays. A program takes and returns all parts, laid end to end along the dimension named above; an argument that names none is the same for every part. Nothing has to cross between parts.
Inputs may be any that keep to these rules, and one draw needn't show every extreme that they name: `temporal_list`: row b lists, in rising order, 2 different frame distances of 1 to 3.
All inputs are finite; a program needn't handle non-finite values.
Results may differ from the reference program's by a relative error of at most 0.012.
Values may be sent and summed in bfloat16 or wider, within the bound.
No kernel may reach another device: no remote copies, remote signals or barrier semaphores. Data moves between devices by JAX's collectives and lax.ppermute only.
A program may use at most 64 MiB of HBM per device.

```python
import math
import jax
import jax.numpy as jnp
from jax import lax

D = 768
HEADS = 8
HEAD_DIM = 96
ACTIONS = 8
PATCHES = 256
DIST = 3
LIST = 2
FRAMES = 8
BLOCK = 128
TOKENS = 2048
QBLOCKS = 16


def drawn_field(key, salt):
    sub_key = jax.random.fold_in(key, salt)
    return jnp.clip(jax.random.normal(sub_key, (FRAMES * PATCHES, D), jnp.float32), -4.5, 4.5)


def draw_queries(key, part):
    return drawn_field(key, 1).astype(jnp.bfloat16)


def draw_keys(key, part):
    return drawn_field(key, 2).astype(jnp.bfloat16)


def draw_temporal_list(key, part):
    skipped = jax.random.randint(jax.random.fold_in(key, 21), (QBLOCKS,), 1, DIST + 1)
    first_skip = jax.random.randint(jax.random.fold_in(key, 22), (), 2, DIST)
    skipped = skipped.at[0].set(first_skip)
    listed = lax.iota(jnp.int32, LIST) + 1
    return listed[None, :] + (listed[None, :] >= skipped[:, None]).astype(jnp.int32)


def plant(entries, own_key, low, top_value):
    longest = entries.shape.index(max(entries.shape))
    spots = []
    for shift in (0, 1):
        where = [jax.random.randint(jax.random.fold_in(own_key, axis), (), 0, length) for axis, length in enumerate(entries.shape)]
        where[longest] = (where[longest] + shift) % entries.shape[longest]
        spots.append(tuple(where))
    return entries.at[spots[0]].set(low).at[spots[1]].set(top_value)


def level_of(own_key, extent, shards, smallest, high):
    level, own = 1.0, jax.random.fold_in(own_key, 6)
    for position, shards_of in shards:
        draws = jnp.exp(jax.random.uniform(jax.random.fold_in(own, position), (shards_of,), jnp.float32, smallest / len(shards), high / len(shards)))
        level = level * jnp.repeat(draws, extent[position] // shards_of).reshape([-1 if axis == position else 1 for axis in range(len(extent))])
    return level


def scatter_about(stream_key, dims, deviation, bound, cuts=(), held_as=jnp.bfloat16):
    drawn = jax.random.normal(stream_key, dims, jnp.float32) * deviation
    if len(cuts) > 0:
        drawn = level_of(stream_key, dims, cuts, -0.22, 0.18) * drawn
    return jnp.clip(drawn, min=-bound, max=bound).astype(held_as)


def setup_inputs(seed: int = 0, part: int = 0) -> dict:
    splits = jax.random.split(jax.random.key(seed), 8)
    part_keys = jax.random.split(jax.random.fold_in(splits[7], part), 8)
    return {
        "queries": draw_queries(jax.random.fold_in(jax.random.fold_in(splits[7], part), 71), part),
        "keys": draw_keys(jax.random.fold_in(jax.random.fold_in(splits[7], part), 71), part),
        "values": scatter_about(part_keys[2], (TOKENS, D), 1.0, 6.0, ((0, 16),)),
        "d_out": scatter_about(part_keys[3], (TOKENS, D), 1.0, 6.0, ((0, 16),)),
        "action_table": scatter_about(splits[4], (ACTIONS, D), 1.0, 5.0),
        "actions": plant(jax.random.randint(part_keys[5], (FRAMES,), 0, ACTIONS), jax.random.fold_in(part_keys[5], 1), 0, ACTIONS - 1).astype(jnp.int32),
        "temporal_list": draw_temporal_list(jax.random.fold_in(jax.random.fold_in(splits[7], part), 71), part),
    }


def attend_block(query_block, key_set, value_set, allowed, grad_block):
    query_rows = query_block.shape[0]
    key_rows = key_set.shape[0]
    score_scale = 1.0 / math.sqrt(HEAD_DIM)
    query_heads = query_block.astype(jnp.float32).reshape(query_rows, HEADS, HEAD_DIM)
    key_heads = key_set.astype(jnp.float32).reshape(key_rows, HEADS, HEAD_DIM)
    value_heads = value_set.astype(jnp.float32).reshape(key_rows, HEADS, HEAD_DIM)
    grad_heads = grad_block.astype(jnp.float32).reshape(query_rows, HEADS, HEAD_DIM)
    scores = jnp.einsum('qhd,khd->hqk', query_heads, key_heads) * score_scale
    scores = jnp.where(allowed[None, None, :], scores, -1e+30)
    highest = lax.optimization_barrier(jnp.max(scores, axis=2, keepdims=True))
    weights = jnp.where(allowed[None, None, :], jnp.exp(scores - highest), 0.0)
    probabilities = weights / lax.optimization_barrier(jnp.sum(weights, axis=2, keepdims=True))
    probs_low = probabilities.astype(jnp.bfloat16).astype(jnp.float32)
    out_full = jnp.einsum('hqk,khd->qhd', probs_low, value_heads)
    d_probs = jnp.einsum('qhd,khd->hqk', grad_heads, value_heads)
    centre = lax.optimization_barrier(jnp.sum(grad_heads * out_full, axis=2))
    d_scores = (probabilities * (d_probs - centre.T[:, :, None])).astype(jnp.bfloat16).astype(jnp.float32)
    grad_query = jnp.einsum('hqk,khd->qhd', d_scores, key_heads) * score_scale
    grad_key = jnp.einsum('hqk,qhd->khd', d_scores, query_heads) * score_scale
    grad_value = jnp.einsum('hqk,qhd->khd', probs_low, grad_heads)
    return (out_full.reshape(query_rows, D), grad_query.reshape(query_rows, D), grad_key.reshape(key_rows, D), grad_value.reshape(key_rows, D))

def add_rows(totals, addition, first_row):
    current = lax.dynamic_slice_in_dim(totals, first_row, addition.shape[0], 0)
    return lax.dynamic_update_slice_in_dim(totals, current + addition, first_row, 0)

def reference(queries, keys, values, d_out, action_table, actions, temporal_list):
    row_blocks = PATCHES // BLOCK
    token_count = FRAMES * PATCHES
    action_rows = jnp.take(action_table, actions, axis=0).astype(jnp.float32)
    cond_values = values.astype(jnp.float32).reshape(FRAMES, PATCHES, D) + action_rows[:, None, :]
    cond_values = cond_values.reshape(token_count, D).astype(jnp.bfloat16)

    def step(carry, block_index):
        key_totals, value_totals = carry
        frame_index = (block_index // row_blocks).astype(jnp.int32)
        row_index = (block_index % row_blocks).astype(jnp.int32)
        query_start = (frame_index * PATCHES + row_index * BLOCK).astype(jnp.int32)
        frame_start = (frame_index * PATCHES).astype(jnp.int32)
        query_block = lax.dynamic_slice_in_dim(queries, query_start, BLOCK, 0)
        grad_block = lax.dynamic_slice_in_dim(d_out, query_start, BLOCK, 0)
        distances = lax.dynamic_index_in_dim(temporal_list, block_index, 0, keepdims=False)
        present = frame_index - distances >= 0
        starts = (jnp.maximum(frame_index - distances, 0) * PATCHES + row_index * BLOCK).astype(jnp.int32)
        key_parts = [lax.dynamic_slice_in_dim(keys, frame_start, PATCHES, 0)]
        value_parts = [lax.dynamic_slice_in_dim(cond_values, frame_start, PATCHES, 0)]
        mask_parts = [jnp.ones((PATCHES,), dtype=bool)]
        for listed in range(LIST):
            key_parts.append(lax.dynamic_slice_in_dim(keys, starts[listed], BLOCK, 0))
            value_parts.append(lax.dynamic_slice_in_dim(cond_values, starts[listed], BLOCK, 0))
            mask_parts.append(jnp.broadcast_to(present[listed], (BLOCK,)))
        key_set = jnp.concatenate(key_parts, axis=0)
        value_set = jnp.concatenate(value_parts, axis=0)
        allowed = jnp.concatenate(mask_parts, axis=0)
        out_full, grad_query, grad_key, grad_value = attend_block(query_block, key_set, value_set, allowed, grad_block)
        key_totals = add_rows(key_totals, grad_key[:PATCHES], frame_start)
        value_totals = add_rows(value_totals, grad_value[:PATCHES], frame_start)
        for listed in range(LIST):
            first_row = PATCHES + listed * BLOCK
            key_totals = add_rows(key_totals, grad_key[first_row:first_row + BLOCK], starts[listed])
            value_totals = add_rows(value_totals, grad_value[first_row:first_row + BLOCK], starts[listed])
        return ((key_totals, value_totals), (out_full.astype(jnp.bfloat16), grad_query.astype(jnp.bfloat16)))
    zero_rows = jnp.zeros((token_count, D), jnp.float32)
    (key_totals, value_totals), (attended, grad_queries) = lax.scan(step, (zero_rows, zero_rows), jnp.arange(QBLOCKS, dtype=jnp.int32))
    attended = attended.reshape(token_count, D)
    grad_queries = grad_queries.reshape(token_count, D)
    frame_sums = lax.optimization_barrier(jnp.sum(value_totals.reshape(FRAMES, PATCHES, D), axis=1))
    selector = (actions[:, None] == jnp.arange(ACTIONS, dtype=jnp.int32)[None, :]).astype(jnp.float32)
    grad_table = jnp.dot(selector.T, frame_sums, precision=lax.Precision.HIGHEST, preferred_element_type=jnp.float32)
    return (attended, grad_queries, key_totals.astype(jnp.bfloat16), value_totals.astype(jnp.bfloat16), grad_table)
```

```python
import math

import jax
import jax.numpy as jnp
from jax import lax
from jax.experimental import pallas as pl
from jax.experimental.pallas import tpu as pltpu
from jax.sharding import PartitionSpec as P

HEADS = 8
HEAD_DIM = 96
LANES = 128
SCALE = 1.0 / math.sqrt(HEAD_DIM)
STAT_ROWS = 24
ACTION_ROWS = 16
MASKED = 1e30
F32 = jnp.float32
BF16 = jnp.bfloat16
VMEM_LIMIT = 56 * 1024 * 1024


def shift(block, distance):
    frames = range(lax.axis_size("tm"))
    return lax.ppermute(block, "tm", [(i - distance, i) for i in frames if i - distance in frames])


def shift_some(block, distance, parity):
    frames = range(lax.axis_size("tm"))
    route = [(i - distance, i) for i in frames if i - distance in frames and i % 2 == parity]
    return lax.ppermute(block, "tm", route)


def swap_pair(block):
    frames = range(lax.axis_size("tm"))
    return lax.ppermute(block, "tm", [(i, i ^ 1) for i in frames if i ^ 1 in frames])


def swap_row(block):
    return lax.ppermute(block, "row", [(0, 1), (1, 0)])


def head_span(head):
    first = head * HEAD_DIM
    low = first // LANES * LANES
    high = -(-(first + HEAD_DIM) // LANES) * LANES
    return slice(low, high), first - low


def own_lanes(block, head):
    span, offset = head_span(head)
    part = block[:, span]
    lane = lax.broadcasted_iota(jnp.int32, part.shape, 1)
    return jnp.where((lane >= offset) & (lane < offset + HEAD_DIM), part, jnp.zeros_like(part))


def join_heads(parts):
    tiles = []
    width = HEADS * HEAD_DIM
    for low in range(0, width, LANES):
        tile = None
        for head in range(HEADS):
            span, offset = head_span(head)
            if span.start <= low < span.stop:
                piece = parts[head][:, low - span.start : low - span.start + LANES]
                if tile is None:
                    tile = piece
                else:
                    lane = lax.broadcasted_iota(jnp.int32, piece.shape, 1) + low
                    tile = jnp.where(lane >= head * HEAD_DIM, piece, tile)
        tiles.append(tile)
    return jnp.concatenate(tiles, axis=1)


def dot_t(left, right):
    return lax.dot_general(left, right, (((1,), (1,)), ((), ())), preferred_element_type=F32)


def dot(left, right):
    return jnp.dot(left, right, preferred_element_type=F32)


def prepare_kernel(actions, queries, keys, values, d_out, table, kv_out, qo_out):
    rows = keys.shape[0]
    action = actions[0]
    chosen = jnp.zeros((1, table.shape[1]), F32)
    for label in range(table.shape[0]):
        row = table[label : label + 1, :].astype(F32)
        chosen = jnp.where(action == label, row, chosen)
    kv_out[0:rows, :] = keys[...]
    kv_out[rows : 2 * rows, :] = (values[...].astype(F32) + chosen).astype(BF16)
    kv_out[2 * rows :, :] = jnp.full((ACTION_ROWS, keys.shape[1]), action.astype(F32), F32).astype(BF16)
    qo_out[0:rows, :] = queries[...]
    qo_out[rows:, :] = d_out[...]


def forward_kernel(frame, listed, qo, own, partner, near2, pair, near3, near1,
                   attended, grad_queries, stats1, stats2, stats3, stats_row, table_out, picked):
    rows = qo.shape[0] // 2
    frame_id = frame[0]
    odd = frame_id % 2
    for slot in range(2):
        distance = listed[0, slot]
        code = jnp.where(distance == 1, jnp.where(odd == 1, 0, 1), distance)
        for value, source in ((0, pair), (1, near1), (2, near2), (3, near3)):
            @pl.when(code == value)
            def _(slot=slot, source=source):
                picked[slot] = source[...]
    present = [frame_id >= listed[0, slot] for slot in range(2)]
    blocks = [own, partner, picked.at[0], picked.at[1]]
    lane = lax.broadcasted_iota(jnp.int32, (rows, LANES), 1)
    columns = jnp.zeros((rows, LANES), F32)
    out_parts, query_parts, sums = [], [], [[], [], []]
    for head in range(HEADS):
        span, _ = head_span(head)
        query = own_lanes(qo[0:rows, :], head)
        grad = own_lanes(qo[rows:, :], head)
        key_blocks = [block[0:rows, span] for block in blocks]
        value_blocks = [block[rows : 2 * rows, span] for block in blocks]
        scores = [dot_t(query, block) * SCALE for block in key_blocks]
        for slot in range(2):
            scores[2 + slot] = jnp.where(present[slot], scores[2 + slot], -MASKED)
        highest = jnp.max(jnp.maximum(jnp.maximum(scores[0], scores[1]), jnp.maximum(scores[2], scores[3])), axis=1, keepdims=True)
        weights = [jnp.exp(block - highest) for block in scores]
        total = jnp.sum(weights[0] + weights[1] + weights[2] + weights[3], axis=1, keepdims=True)
        inverse = 1.0 / total
        probs = [block * inverse for block in weights]
        probs_low = [block.astype(BF16) for block in probs]
        rounded = [block.astype(F32) for block in probs_low]
        d_probs = [dot_t(grad, block) for block in value_blocks]
        centre = jnp.sum(rounded[0] * d_probs[0] + rounded[1] * d_probs[1] + rounded[2] * d_probs[2] + rounded[3] * d_probs[3], axis=1, keepdims=True)
        d_scores = [(p * (d - centre)).astype(BF16) for p, d in zip(probs, d_probs)]
        out_parts.append(sum(dot(p, v) for p, v in zip(probs_low, value_blocks)))
        query_parts.append(sum(dot(d, k) for d, k in zip(d_scores, key_blocks)))
        columns = jnp.where(lane == head, highest + jnp.log(total), columns)
        columns = jnp.where(lane == HEADS + head, centre, columns)
        wide = grad.astype(F32)
        masses = (rounded[0] + rounded[1], rounded[2], rounded[3])
        for group in range(3):
            mass = jnp.sum(masses[group], axis=1, keepdims=True)
            sums[group].append(jnp.sum(wide * mass, axis=0, keepdims=True))
    attended[...] = join_heads(out_parts).astype(BF16)
    grad_queries[...] = (join_heads(query_parts) * SCALE).astype(BF16)
    turned = columns.T
    for distance, stats in ((1, stats1), (2, stats2), (3, stats3)):
        in_list = (listed[0, 0] == distance) | (listed[0, 1] == distance)
        stats[0 : 2 * HEADS, :] = turned[0 : 2 * HEADS, :]
        stats[2 * HEADS :, :] = jnp.full((HEADS, LANES), jnp.where(in_list, 1.0, 0.0), F32)
    stats_row[...] = turned[0 : 2 * HEADS, :]
    label = lax.broadcasted_iota(jnp.int32, table_out.shape, 0).astype(F32)
    totals = jnp.zeros(table_out.shape, F32)
    for group, block in ((0, own), (1, picked.at[0]), (2, picked.at[1])):
        action = block[2 * rows :, :].astype(F32)[0:1, :]
        addend = join_heads(sums[group])
        totals = totals + jnp.where(label == action, addend, 0.0)
    table_out[...] = totals


def backward_kernel(frame, own, qo, qo_partner, late2, late_pair, late3, late1,
                    stats_own, stats_partner, stats1, stats2, stats3, grad_keys, grad_values):
    rows = qo.shape[0] // 2
    odd = frame[0] % 2
    key_parts, value_parts = [], []
    first = jnp.where(odd == 1, late1[...], late_pair[...])
    queries = [qo[0:rows, :], qo_partner[0:rows, :], first[0:rows, :], late2[0:rows, :], late3[0:rows, :]]
    grads = [qo[rows:, :], qo_partner[rows:, :], first[rows:, :], late2[rows:, :], late3[rows:, :]]
    queries = jnp.concatenate(queries, axis=0)
    grads = jnp.concatenate(grads, axis=0)
    late = []
    for stats in (stats1, stats2, stats3):
        late.append(jnp.where(stats[2 * HEADS :, :] > 0.5, stats[0:HEADS, :], MASKED))
    log_totals = jnp.concatenate([stats_own[0:HEADS, :], stats_partner[0:HEADS, :]] + late, axis=1)
    centres = jnp.concatenate([s[HEADS : 2 * HEADS, :] for s in (stats_own, stats_partner, stats1, stats2, stats3)], axis=1)
    for head in range(HEADS):
        span, _ = head_span(head)
        key = own_lanes(own[0:rows, :], head)
        value = own_lanes(own[rows : 2 * rows, :], head)
        scores = dot_t(key, queries[:, span]) * SCALE
        probs = jnp.exp(scores - log_totals[head : head + 1, :])
        d_probs = dot_t(value, grads[:, span])
        d_scores = (probs * (d_probs - centres[head : head + 1, :])).astype(BF16)
        value_parts.append(dot(probs.astype(BF16), grads[:, span]))
        key_parts.append(dot(d_scores, queries[:, span]))
    grad_keys[...] = (join_heads(key_parts) * SCALE).astype(BF16)
    grad_values[...] = join_heads(value_parts).astype(BF16)


def vmem(count):
    return [pl.BlockSpec(memory_space=pltpu.VMEM)] * count


def smem(count):
    return [pl.BlockSpec(memory_space=pltpu.SMEM)] * count


def params():
    return pltpu.CompilerParams(vmem_limit_bytes=VMEM_LIMIT)


def sum_table(table):
    frames = lax.axis_size("tm")
    if frames & (frames - 1):
        return lax.psum(table, ("tm", "row"))
    table = table + swap_row(table)
    step = 1
    while step < frames:
        table = table + lax.ppermute(table, "tm", [(i, i ^ step) for i in range(frames)])
        step *= 2
    return table


def on_device(queries, keys, values, d_out, action_table, actions, temporal_list):
    rows, width = queries.shape
    frame = lax.axis_index("tm").astype(jnp.int32).reshape(1)
    shape = jax.ShapeDtypeStruct
    kv, qo = pl.pallas_call(
        prepare_kernel,
        out_shape=(shape((2 * rows + ACTION_ROWS, width), BF16), shape((2 * rows, width), BF16)),
        in_specs=smem(1) + vmem(5),
        out_specs=vmem(2),
        compiler_params=params(),
    )(actions, queries, keys, values, d_out, action_table)
    near2 = shift(kv, 2)
    pair = swap_pair(kv)
    partner = swap_row(kv)
    near3 = shift(near2, 1)
    near1 = shift_some(pair, 2, 0)
    late2 = shift(qo, -2)
    late_pair = swap_pair(qo)
    qo_partner = swap_row(qo)
    late3 = shift(late2, -1)
    late1 = shift_some(late_pair, -2, 1)
    attended, grad_queries, stats1, stats2, stats3, stats_row, table = pl.pallas_call(
        forward_kernel,
        out_shape=(
            shape((rows, width), BF16),
            shape((rows, width), BF16),
            shape((STAT_ROWS, LANES), F32),
            shape((STAT_ROWS, LANES), F32),
            shape((STAT_ROWS, LANES), F32),
            shape((2 * HEADS, LANES), F32),
            shape(action_table.shape, F32),
        ),
        in_specs=smem(2) + vmem(7),
        out_specs=vmem(7),
        scratch_shapes=[pltpu.VMEM((2, 2 * rows + ACTION_ROWS, width), BF16)],
        compiler_params=params(),
    )(frame, temporal_list, qo, kv, partner, near2, pair, near3, near1)
    late_stats = [shift(stats, -distance) for distance, stats in ((1, stats1), (2, stats2), (3, stats3))]
    stats_partner = swap_row(stats_row)
    grad_table = sum_table(table)
    grad_keys, grad_values = pl.pallas_call(
        backward_kernel,
        out_shape=(shape((rows, width), BF16), shape((rows, width), BF16)),
        in_specs=smem(1) + vmem(12),
        out_specs=vmem(2),
        compiler_params=params(),
    )(frame, kv, qo, qo_partner, late2, late_pair, late3, late1, stats_row, stats_partner, *late_stats)
    return attended, grad_queries, grad_keys, grad_values, grad_table


def solution(mesh):
    split = P(("grp", "tm", "row"), None)
    return jax.shard_map(
        on_device,
        mesh=mesh,
        in_specs=(split, split, split, split, P(), P(("grp", "tm")), split),
        out_specs=(split, split, split, split, P("grp", None)),
        check_vma=False,
    )
```

```python
import math

import jax
import jax.numpy as jnp
from jax import lax
from jax.experimental import pallas as pl
from jax.experimental.pallas import tpu as pltpu
from jax.sharding import PartitionSpec as P

HEADS = 8
HEAD_DIM = 96
LANES = 128
SCALE = 1.0 / math.sqrt(HEAD_DIM)
STAT_ROWS = 24
ACTIONS = 8
EXP2_SCALE = SCALE * math.log2(math.e)
ACTION_ROWS = 16
MASKED = 1e30
F32 = jnp.float32
BF16 = jnp.bfloat16
VMEM_LIMIT = 56 * 1024 * 1024


def shift(block, distance):
    frames = range(lax.axis_size("tm"))
    return lax.ppermute(block, "tm", [(i - distance, i) for i in frames if i - distance in frames])


def shift_some(block, distance, parity):
    frames = range(lax.axis_size("tm"))
    route = [(i - distance, i) for i in frames if i - distance in frames and i % 2 == parity]
    return lax.ppermute(block, "tm", route)


def swap_pair(block):
    frames = range(lax.axis_size("tm"))
    return lax.ppermute(block, "tm", [(i, i ^ 1) for i in frames if i ^ 1 in frames])


def swap_row(block):
    return lax.ppermute(block, "row", [(0, 1), (1, 0)])


def pair_span(pair):
    first = 2 * pair * HEAD_DIM
    low = first // LANES * LANES
    high = -(-(first + 2 * HEAD_DIM) // LANES) * LANES
    return slice(low, high), (first - low, first - low + HEAD_DIM)


def split_pair(part, starts):
    lane = lax.broadcasted_iota(jnp.int32, part.shape, 1)
    none = jnp.zeros_like(part)
    return jnp.concatenate([jnp.where((lane >= start) & (lane < start + HEAD_DIM), part, none) for start in starts], axis=0)


def merge_pair(stacked, starts):
    half = stacked.shape[0] // 2
    lane = lax.broadcasted_iota(jnp.int32, (half, stacked.shape[1]), 1)
    return jnp.where(lane < starts[1], stacked[0:half], stacked[half:])


def join_pairs(parts):
    tiles = []
    for low in range(0, HEADS * HEAD_DIM, LANES):
        tile = None
        for pair in range(HEADS // 2):
            span, _ = pair_span(pair)
            if span.start <= low < span.stop:
                piece = parts[pair][:, low - span.start : low - span.start + LANES]
                if tile is None:
                    tile = piece
                else:
                    lane = lax.broadcasted_iota(jnp.int32, piece.shape, 1) + low
                    tile = jnp.where(lane >= 2 * pair * HEAD_DIM, piece, tile)
        tiles.append(tile)
    return tiles


def dot_t(left, right):
    return lax.dot_general(left, right, (((1,), (1,)), ((), ())), preferred_element_type=F32)


def dot(left, right):
    return jnp.dot(left, right, preferred_element_type=F32)


def prepare_kernel(actions, keys, values, table, queries, d_out, kv, qo):
    rows = values.shape[0]
    action = actions[0]
    chosen = jnp.zeros((1, table.shape[1]), F32)
    for label in range(table.shape[0]):
        row = table[label : label + 1, :].astype(F32)
        chosen = jnp.where(action == label, row, chosen)
    kv[0:rows, :] = keys[...]
    kv[rows : 2 * rows, :] = (values[...].astype(F32) + chosen).astype(BF16)
    kv[2 * rows :, :] = jnp.full((ACTION_ROWS, values.shape[1]), action.astype(F32), F32).astype(BF16)
    qo[0:rows, :] = queries[...]
    qo[rows:, :] = d_out[...]


def forward_kernel(frame, listed, queries, d_out, own, partner, near2, pair, near3, near1,
                   attended, grad_queries, row_message, all_k, all_v):
    rows = queries.shape[0]
    frame_id = frame[0]
    odd = frame_id % 2
    for index, source in ((0, own), (1, partner)):
        all_k[index * rows : (index + 1) * rows, :] = source[0:rows, :]
        all_v[index * rows : (index + 1) * rows, :] = source[rows : 2 * rows, :]
    present = []
    for slot in range(2):
        distance = listed[0, slot]
        code = jnp.where(distance == 1, jnp.where(odd == 1, 0, 1), distance)
        begin = (2 + slot) * rows
        for value, source in ((0, pair), (1, near1), (2, near2), (3, near3)):
            @pl.when(code == value)
            def _(begin=begin, source=source, slot=slot):
                all_k[begin : begin + rows, :] = source[0:rows, :]
                all_v[begin : begin + rows, :] = source[rows : 2 * rows, :]
                all_v[(4 * rows + slot * ACTION_ROWS) : (4 * rows + (slot + 1) * ACTION_ROWS), :] = source[2 * rows :, :]
        present.append(frame_id >= distance)
    lane = lax.broadcasted_iota(jnp.int32, (rows, LANES), 1)
    group_row = lax.broadcasted_iota(jnp.int32, (4 * rows, LANES), 0) // rows
    group_lane = lax.broadcasted_iota(jnp.int32, (4 * rows, LANES), 1)
    members = (jnp.maximum(group_row - 1, 0) == group_lane).astype(BF16)
    columns = jnp.zeros((rows, LANES), F32)
    out_parts, query_parts, sums = [], [], [[], [], []]
    for pair in range(HEADS // 2):
        span, starts = pair_span(pair)
        query = split_pair(queries[:, span], starts)
        grad = split_pair(d_out[:, span], starts)
        key = all_k[0 : 4 * rows, span]
        value = all_v[0 : 4 * rows, span]
        scores = dot_t(query, key)
        scores = [scores[:, 0 : 2 * rows]] + [
            jnp.where(present[slot], scores[:, (2 + slot) * rows : (3 + slot) * rows], -MASKED) for slot in range(2)
        ]
        scores = jnp.concatenate(scores, axis=1)
        highest = jnp.max(scores, axis=1, keepdims=True)
        weights = jnp.exp2((scores - highest) * EXP2_SCALE)
        total = jnp.sum(weights, axis=1, keepdims=True)
        probs = weights * (1.0 / total)
        probs_low = probs.astype(BF16)
        out = dot(probs_low, value)
        d_probs = dot_t(grad, value)
        wide = grad.astype(F32)
        centre = jnp.sum(wide * out, axis=1, keepdims=True)
        d_scores = (probs * (d_probs - centre)).astype(BF16)
        out_parts.append(merge_pair(out, starts))
        query_parts.append(merge_pair(dot(d_scores, key), starts))
        log_total = highest * EXP2_SCALE + jnp.log2(total)
        for half in range(2):
            picked = slice(half * rows, (half + 1) * rows)
            columns = jnp.where(lane == 2 * pair + half, log_total[picked], columns)
            columns = jnp.where(lane == HEADS + 2 * pair + half, centre[picked], columns)
        mass = dot(probs_low, members)
        for group in range(3):
            sums[group].append(jnp.sum(wide * mass[:, group : group + 1], axis=0, keepdims=True))
    out_tiles, query_tiles = join_pairs(out_parts), join_pairs(query_parts)
    attended[...] = jnp.concatenate(out_tiles, axis=1).astype(BF16)
    grad_queries[...] = (jnp.concatenate(query_tiles, axis=1) * SCALE).astype(BF16)
    turned = columns.T
    row_message[0 : 2 * HEADS, :] = turned[0 : 2 * HEADS, :]
    which = lax.broadcasted_iota(jnp.int32, (HEADS, LANES), 0)
    in_list = (which == listed[0, 0]) | (which == listed[0, 1])
    row_message[2 * HEADS : STAT_ROWS, :] = jnp.where(in_list, 1.0, 0.0)
    tiles = [add_pairs(parts) for parts in sums]
    label = lax.broadcasted_iota(jnp.int32, (ACTIONS, LANES), 0).astype(F32)
    for index in range(len(tiles[0])):
        totals = jnp.zeros((ACTIONS, LANES), F32)
        cut = slice(index * LANES, (index + 1) * LANES)
        actions = [own[2 * rows :, cut]]
        actions += [all_v[4 * rows + slot * ACTION_ROWS : 4 * rows + (slot + 1) * ACTION_ROWS, cut] for slot in range(2)]
        for group in range(3):
            action = actions[group].astype(F32)[0:1, :]
            totals = totals + jnp.where(label == action, tiles[group][index], 0.0)
        row_message[STAT_ROWS + index * ACTIONS : STAT_ROWS + (index + 1) * ACTIONS, :] = totals


def add_pairs(parts):
    tiles = []
    for low in range(0, HEADS * HEAD_DIM, LANES):
        tile = None
        for pair in range(HEADS // 2):
            span, _ = pair_span(pair)
            if span.start <= low < span.stop:
                piece = parts[pair][:, low - span.start : low - span.start + LANES]
                tile = piece if tile is None else tile + piece
        tiles.append(tile)
    return tiles


def backward_pairs(own, queries, grads, log_totals, centres):
    rows = (own.shape[0] - ACTION_ROWS) // 2
    key_parts, value_parts = [], []
    for pair in range(HEADS // 2):
        span, starts = pair_span(pair)
        key = split_pair(own[0:rows, span], starts)
        value = split_pair(own[rows : 2 * rows, span], starts)
        query = queries[:, span]
        grad = grads[:, span]
        scores = dot_t(key, query)
        d_probs = dot_t(value, grad)
        low, d_low = [], []
        for half in range(2):
            head = 2 * pair + half
            cut = slice(half * rows, (half + 1) * rows)
            probs = jnp.exp2(scores[cut] * EXP2_SCALE - log_totals[head : head + 1, :])
            low.append(probs.astype(BF16))
            d_low.append((probs * (d_probs[cut] - centres[head : head + 1, :])).astype(BF16))
        value_parts.append(merge_pair(dot(jnp.concatenate(low, axis=0), grad), starts))
        key_parts.append(merge_pair(dot(jnp.concatenate(d_low, axis=0), query), starts))
    return jnp.concatenate(join_pairs(key_parts), axis=1), jnp.concatenate(join_pairs(value_parts), axis=1)


def near_backward_kernel(own, qo, qo_partner, row_own, row_partner, near_keys, near_values, all_q, all_g):
    rows = qo.shape[0] // 2
    for index, source in ((0, qo), (1, qo_partner)):
        all_q[index * rows : (index + 1) * rows, :] = source[0:rows, :]
        all_g[index * rows : (index + 1) * rows, :] = source[rows:, :]
    log_totals = jnp.concatenate([row_own[0:HEADS, :], row_partner[0:HEADS, :]], axis=1)
    centres = jnp.concatenate([row_own[HEADS : 2 * HEADS, :], row_partner[HEADS : 2 * HEADS, :]], axis=1)
    near_keys[...], near_values[...] = backward_pairs(own, all_q, all_g, log_totals, centres)


def far_backward_kernel(frame, own, late2, late_pair, late3, late1, stats, near_keys, near_values,
                        grad_keys, grad_values, all_q, all_g):
    rows = late2.shape[0] // 2
    frame_id = frame[0]
    odd = frame_id % 2
    for index, source in ((1, late2), (2, late3)):
        all_q[index * rows : (index + 1) * rows, :] = source[0:rows, :]
        all_g[index * rows : (index + 1) * rows, :] = source[rows:, :]
    for value, source in ((0, late_pair), (1, late1)):
        @pl.when(odd == value)
        def _(source=source):
            all_q[0:rows, :] = source[0:rows, :]
            all_g[0:rows, :] = source[rows:, :]
    log_totals, centres = [], []
    for distance in (1, 2, 3):
        later = frame_id + distance
        exists = later < stats.shape[0]
        block = stats[jnp.where(exists, later ^ frame_id, 0)]
        uses = exists & (block[2 * HEADS + distance : 2 * HEADS + distance + 1, :] > 0.5)
        log_totals.append(jnp.where(uses, block[0:HEADS, :], MASKED))
        centres.append(block[HEADS : 2 * HEADS, :])
    log_totals = jnp.concatenate(log_totals, axis=1)
    centres = jnp.concatenate(centres, axis=1)
    far_keys, far_values = backward_pairs(own, all_q, all_g, log_totals, centres)
    grad_keys[...] = ((near_keys[...] + far_keys) * SCALE).astype(BF16)
    grad_values[...] = (near_values[...] + far_values).astype(BF16)


def vmem(count):
    return [pl.BlockSpec(memory_space=pltpu.VMEM)] * count


def smem(count):
    return [pl.BlockSpec(memory_space=pltpu.SMEM)] * count


def params():
    return pltpu.CompilerParams(vmem_limit_bytes=VMEM_LIMIT)


def call(kernel, outs, scalars, arrays, scratch=()):
    return pl.pallas_call(
        kernel,
        out_shape=outs,
        in_specs=smem(len(scalars)) + vmem(len(arrays)),
        out_specs=jax.tree.map(lambda _: pl.BlockSpec(memory_space=pltpu.VMEM), outs),
        scratch_shapes=list(scratch),
        compiler_params=params(),
        cost_estimate=pl.CostEstimate(flops=100000000000, transcendentals=1, bytes_accessed=1000),
    )(*scalars, *arrays)


def share(message):
    frames = lax.axis_size("tm")
    stats, table = message[:STAT_ROWS], message[STAT_ROWS:]
    gathered = stats[None]
    if frames & (frames - 1):
        around = lax.all_gather(stats, "tm")
        order = lax.iota(jnp.int32, 1 << (frames - 1).bit_length()) ^ lax.axis_index("tm").astype(jnp.int32)
        return lax.psum(table, "tm"), jnp.take(around, jnp.minimum(order, frames - 1), axis=0)
    step = 1
    while step < frames:
        if step > 1:
            message = jnp.concatenate([gathered.reshape(-1, LANES), table])
        message = lax.ppermute(message, "tm", [(i, i ^ step) for i in range(frames)])
        table = table + message[step * STAT_ROWS :]
        gathered = jnp.concatenate([gathered, message[: step * STAT_ROWS].reshape(gathered.shape)])
        step *= 2
    return table, gathered


def on_device(queries, keys, values, d_out, action_table, actions, temporal_list):
    rows, width = queries.shape
    tiles = width // LANES
    frame = lax.axis_index("tm").astype(jnp.int32).reshape(1)
    shape = jax.ShapeDtypeStruct
    kv, qo = call(
        prepare_kernel,
        (shape((2 * rows + ACTION_ROWS, width), BF16), shape((2 * rows, width), BF16)),
        [actions],
        [keys, values, action_table, queries, d_out],
    )
    near2, pair = shift(kv, 2), swap_pair(kv)
    late2, late_pair = shift(qo, -2), swap_pair(qo)
    partner, qo_partner = swap_row(kv), swap_row(qo)
    near3, near1 = shift(near2, 1), shift_some(pair, 2, 0)
    late3 = shift(late2, -1)
    late1 = shift_some(late_pair, -2, 1)
    attended, grad_queries, row_message = call(
        forward_kernel,
        (
            shape((rows, width), BF16),
            shape((rows, width), BF16),
            shape((STAT_ROWS + tiles * ACTIONS, LANES), F32),
        ),
        [frame, temporal_list],
        [queries, d_out, kv, partner, near2, pair, near3, near1],
        [pltpu.VMEM((4 * rows, width), BF16), pltpu.VMEM((4 * rows + 2 * ACTION_ROWS, width), BF16)],
    )
    row_partner = swap_row(row_message[:STAT_ROWS])
    table, stats = share(row_message)
    table = table + swap_row(table)
    near_keys, near_values = call(
        near_backward_kernel,
        (shape((rows, width), F32), shape((rows, width), F32)),
        [],
        [kv, qo, qo_partner, row_message, row_partner],
        [pltpu.VMEM((2 * rows, width), BF16), pltpu.VMEM((2 * rows, width), BF16)],
    )
    grad_table = table.reshape(tiles, ACTIONS, LANES).transpose(1, 0, 2).reshape(ACTIONS, width)
    grad_keys, grad_values = call(
        far_backward_kernel,
        (shape((rows, width), BF16), shape((rows, width), BF16)),
        [frame],
        [kv, late2, late_pair, late3, late1, stats, near_keys, near_values],
        [pltpu.VMEM((3 * rows, width), BF16), pltpu.VMEM((3 * rows, width), BF16)],
    )
    return attended, grad_queries, grad_keys, grad_values, grad_table


def solution(mesh):
    split = P(("grp", "tm", "row"), None)
    return jax.shard_map(
        on_device,
        mesh=mesh,
        in_specs=(split, split, split, split, P(), P(("grp", "tm")), split),
        out_specs=(split, split, split, split, P("grp", None)),
        check_vma=False,
    )
```

```python
import math

import jax
import jax.numpy as jnp
from jax import lax
from jax.experimental import pallas as pl
from jax.experimental.pallas import tpu as pltpu
from jax.sharding import PartitionSpec as P

HEADS = 8
HEAD_DIM = 96
LANES = 128
SCALE = 1.0 / math.sqrt(HEAD_DIM)
STAT_ROWS = 24
HOLD = True
PREP, FWD, NEAR, FAR, QUERY = 10**11, 10**10, 10**9, 10**11, 10**9
GROUP_ROWS = 16
ACTIONS = 8
EXP2_SCALE = SCALE * math.log2(math.e)
ACTION_ROWS = 16
MASKED = 1e30
F32 = jnp.float32
BF16 = jnp.bfloat16
VMEM_LIMIT = 56 * 1024 * 1024


def shift(block, distance):
    frames = range(lax.axis_size("tm"))
    return lax.ppermute(block, "tm", [(i - distance, i) for i in frames if i - distance in frames])


def shift_some(block, distance, parity):
    frames = range(lax.axis_size("tm"))
    route = [(i - distance, i) for i in frames if i - distance in frames and i % 2 == parity]
    return lax.ppermute(block, "tm", route)


def swap_pair(block):
    frames = range(lax.axis_size("tm"))
    return lax.ppermute(block, "tm", [(i, i ^ 1) for i in frames if i ^ 1 in frames])


def swap_row(block):
    return lax.ppermute(block, "row", [(0, 1), (1, 0)])


def pair_span(pair):
    first = 2 * pair * HEAD_DIM
    low = first // LANES * LANES
    high = -(-(first + 2 * HEAD_DIM) // LANES) * LANES
    return slice(low, high), (first - low, first - low + HEAD_DIM)


def split_pair(part, starts):
    lane = lax.broadcasted_iota(jnp.int32, part.shape, 1)
    none = jnp.zeros_like(part)
    return jnp.concatenate([jnp.where((lane >= start) & (lane < start + HEAD_DIM), part, none) for start in starts], axis=0)


def merge_pair(stacked, starts):
    half = stacked.shape[0] // 2
    lane = lax.broadcasted_iota(jnp.int32, (half, stacked.shape[1]), 1)
    return jnp.where(lane < starts[1], stacked[0:half], stacked[half:])


def join_pairs(parts):
    tiles = []
    for low in range(0, HEADS * HEAD_DIM, LANES):
        tile = None
        for pair in range(HEADS // 2):
            span, _ = pair_span(pair)
            if span.start <= low < span.stop:
                piece = parts[pair][:, low - span.start : low - span.start + LANES]
                if tile is None:
                    tile = piece
                else:
                    lane = lax.broadcasted_iota(jnp.int32, piece.shape, 1) + low
                    tile = jnp.where(lane >= 2 * pair * HEAD_DIM, piece, tile)
        tiles.append(tile)
    return tiles


def dot_t(left, right):
    return lax.dot_general(left, right, (((1,), (1,)), ((), ())), preferred_element_type=F32)


def dot(left, right):
    return jnp.dot(left, right, preferred_element_type=F32)


def prepare_kernel(actions, keys, values, table, queries, d_out, kv, qo):
    rows = values.shape[0]
    action = actions[...]
    label = lax.broadcasted_iota(jnp.int32, table.shape, 0)
    chosen = jnp.sum(jnp.where(label == action, table[...].astype(F32), 0.0), axis=0, keepdims=True)
    kv[0:rows, :] = keys[...]
    kv[rows : 2 * rows, :] = (values[...].astype(F32) + chosen).astype(BF16)
    kv[2 * rows :, :] = jnp.broadcast_to(action.astype(F32), (ACTION_ROWS, values.shape[1])).astype(BF16)
    qo[0:rows, :] = queries[...]
    qo[rows:, :] = d_out[...]


def forward_kernel(frame, listed, own_action, queries, d_out, own, partner, near2, pair, near3, near1,
                   row_message, attended, d_low, picked):
    rows = queries.shape[0]
    frame_id = frame[0]
    odd = frame_id % 2
    present = []
    for slot in range(2):
        distance = listed[0, slot]
        code = jnp.where(distance == 1, jnp.where(odd == 1, 0, 1), distance)
        for value, source in ((0, pair), (1, near1), (2, near2), (3, near3)):
            @pl.when(code == value)
            def _(source=source, slot=slot):
                picked[slot] = source[...]
        present.append(frame_id >= distance)
    blocks = [own, partner, picked.at[0], picked.at[1]]
    lane = lax.broadcasted_iota(jnp.int32, (rows, LANES), 1)
    member_row = lax.broadcasted_iota(jnp.int32, (GROUP_ROWS, 4 * rows), 0)
    member_block = lax.broadcasted_iota(jnp.int32, (GROUP_ROWS, 4 * rows), 1) // rows
    members = jnp.where(jnp.maximum(member_block - 1, 0) == member_row, 1.0, 0.0).astype(BF16)
    columns = jnp.zeros((rows, LANES), F32)
    out_parts, sums = [], [[], [], []]
    for pair in range(HEADS // 2):
        span, starts = pair_span(pair)
        query = split_pair(queries[:, span], starts)
        grad = split_pair(d_out[:, span], starts)
        key = jnp.concatenate([block[0:rows, span] for block in blocks], axis=0)
        value = jnp.concatenate([block[rows : 2 * rows, span] for block in blocks], axis=0)
        scores = dot_t(query, key)
        scores = [scores[:, 0 : 2 * rows]] + [
            jnp.where(present[slot], scores[:, (2 + slot) * rows : (3 + slot) * rows], -MASKED) for slot in range(2)
        ]
        scores = jnp.concatenate(scores, axis=1)
        highest = jnp.max(scores, axis=1, keepdims=True)
        weights = jnp.exp2((scores - highest) * EXP2_SCALE)
        total = jnp.sum(weights, axis=1, keepdims=True)
        probs = weights * (1.0 / total)
        probs_low = probs.astype(BF16)
        out = dot(probs_low, value)
        d_probs = dot_t(grad, value)
        centre = jnp.sum(grad.astype(F32) * out, axis=1, keepdims=True)
        d_low[pair] = (probs * (d_probs - centre)).astype(BF16)
        out_parts.append(merge_pair(out, starts))
        log_total = highest * EXP2_SCALE + jnp.log2(total)
        for half in range(2):
            cut = slice(half * rows, (half + 1) * rows)
            columns = jnp.where(lane == 2 * pair + half, log_total[cut], columns)
            columns = jnp.where(lane == HEADS + 2 * pair + half, centre[cut], columns)
        mass = dot_t(members, probs_low)
        mass_high = mass.astype(BF16)
        mass_low = (mass - mass_high.astype(F32)).astype(BF16)
        weighted = dot(jnp.concatenate([mass_high, mass_low], axis=0), grad)
        weighted = weighted[0:GROUP_ROWS] + weighted[GROUP_ROWS:]
        for group in range(3):
            sums[group].append(weighted[group : group + 1])
    attended[...] = jnp.concatenate(join_pairs(out_parts), axis=1).astype(BF16)
    turned = columns.T
    row_message[0 : 2 * HEADS, :] = turned[0 : 2 * HEADS, :]
    which = lax.broadcasted_iota(jnp.int32, (HEADS, LANES), 0)
    in_list = (which == listed[0, 0]) | (which == listed[0, 1])
    row_message[2 * HEADS : STAT_ROWS, :] = jnp.where(in_list, 1.0, 0.0)
    tiles = [add_pairs(parts) for parts in sums]
    label = lax.broadcasted_iota(jnp.int32, (ACTIONS, LANES), 0).astype(F32)
    for index in range(len(tiles[0])):
        totals = jnp.zeros((ACTIONS, LANES), F32)
        cut = slice(index * LANES, (index + 1) * LANES)
        actions = [own_action[0].astype(F32)] + [picked[slot, 2 * rows :, cut].astype(F32)[0:1, :] for slot in range(2)]
        for group in range(3):
            action = actions[group]
            totals = totals + jnp.where(label == action, tiles[group][index], 0.0)
        row_message[STAT_ROWS + index * ACTIONS : STAT_ROWS + (index + 1) * ACTIONS, :] = totals


def query_kernel(own, partner, picked, d_low, held, attended, grad_queries):
    rows = held.shape[0]
    parts = []
    for pair in range(HEADS // 2):
        span, starts = pair_span(pair)
        key = jnp.concatenate([block[0:rows, span] for block in (own, partner, picked.at[0], picked.at[1])], axis=0)
        parts.append(merge_pair(dot(d_low[pair], key), starts))
    grad_queries[...] = (jnp.concatenate(join_pairs(parts), axis=1) * SCALE).astype(BF16)
    attended[...] = held[...]


def add_pairs(parts):
    tiles = []
    for low in range(0, HEADS * HEAD_DIM, LANES):
        tile = None
        for pair in range(HEADS // 2):
            span, _ = pair_span(pair)
            if span.start <= low < span.stop:
                piece = parts[pair][:, low - span.start : low - span.start + LANES]
                tile = piece if tile is None else tile + piece
        tiles.append(tile)
    return tiles


def backward_pairs(own, sources, log_totals, centres):
    rows = (own.shape[0] - ACTION_ROWS) // 2
    key_parts, value_parts = [], []
    for pair in range(HEADS // 2):
        span, starts = pair_span(pair)
        key = split_pair(own[0:rows, span], starts)
        value = split_pair(own[rows : 2 * rows, span], starts)
        query = jnp.concatenate([source(slice(0, rows), span) for source in sources], axis=0)
        grad = jnp.concatenate([source(slice(rows, 2 * rows), span) for source in sources], axis=0)
        scores = dot_t(key, query)
        d_probs = dot_t(value, grad)
        low, d_low = [], []
        for half in range(2):
            head = 2 * pair + half
            cut = slice(half * rows, (half + 1) * rows)
            probs = jnp.exp2(scores[cut] * EXP2_SCALE - log_totals[head : head + 1, :])
            low.append(probs.astype(BF16))
            d_low.append((probs * (d_probs[cut] - centres[head : head + 1, :])).astype(BF16))
        value_parts.append(merge_pair(dot(jnp.concatenate(low, axis=0), grad), starts))
        key_parts.append(merge_pair(dot(jnp.concatenate(d_low, axis=0), query), starts))
    return jnp.concatenate(join_pairs(key_parts), axis=1), jnp.concatenate(join_pairs(value_parts), axis=1)


def reader(ref):
    return lambda rows, lanes: ref[rows, lanes]


def near_backward_kernel(own, row_own, row_partner, qo, qo_partner, near_keys, near_values):
    log_totals = jnp.concatenate([row_own[0:HEADS, :], row_partner[0:HEADS, :]], axis=1)
    centres = jnp.concatenate([row_own[HEADS : 2 * HEADS, :], row_partner[HEADS : 2 * HEADS, :]], axis=1)
    sources = [reader(qo), reader(qo_partner)]
    near_keys[...], near_values[...] = backward_pairs(own, sources, log_totals, centres)


def reverse_bits(index, count):
    bits = (count - 1).bit_length()
    return sum(((index >> bit) & 1) << (bits - 1 - bit) for bit in range(bits))


def far_backward_kernel(frame, own, stats, near_keys, near_values, late2, late_pair, late3, late1,
                        grad_keys, grad_values):
    frame_id = frame[0]
    odd = frame_id % 2 == 1
    sources = [lambda rows, lanes: jnp.where(odd, late1[rows, lanes], late_pair[rows, lanes]), reader(late2), reader(late3)]
    log_totals, centres = [], []
    for distance in (1, 2, 3):
        later = frame_id + distance
        exists = later < stats.shape[0]
        block = stats[jnp.where(exists, reverse_bits(later ^ frame_id, stats.shape[0]), 0)]
        uses = exists & (block[2 * HEADS + distance : 2 * HEADS + distance + 1, :] > 0.5)
        log_totals.append(jnp.where(uses, block[0:HEADS, :], MASKED))
        centres.append(block[HEADS : 2 * HEADS, :])
    log_totals = jnp.concatenate(log_totals, axis=1)
    centres = jnp.concatenate(centres, axis=1)
    far_keys, far_values = backward_pairs(own, sources, log_totals, centres)
    grad_keys[...] = ((near_keys[...] + far_keys) * SCALE).astype(BF16)
    grad_values[...] = (near_values[...] + far_values).astype(BF16)


VMEM, SMEM = pltpu.VMEM, pltpu.SMEM


def call(kernel, flops, outs, scalars, arrays, scratch=()):
    return pl.pallas_call(
        kernel,
        out_shape=tuple(pltpu.VMEM(shape, dtype) if stays else jax.ShapeDtypeStruct(shape, dtype) for shape, dtype, stays in outs),
        in_specs=[pl.BlockSpec(memory_space=SMEM)] * len(scalars) + [pl.BlockSpec(memory_space=VMEM)] * len(arrays),
        out_specs=(pl.BlockSpec(memory_space=VMEM),) * len(outs),
        scratch_shapes=list(scratch),
        compiler_params=pltpu.CompilerParams(vmem_limit_bytes=VMEM_LIMIT),
        cost_estimate=pl.CostEstimate(flops=flops, transcendentals=0, bytes_accessed=0),
    )(*scalars, *[pltpu.with_memory_space_constraint(array, VMEM) if hold else array for array, hold in arrays])


def share(message):
    frames = lax.axis_size("tm")
    stats, table = message[:STAT_ROWS], message[STAT_ROWS:]
    gathered = stats[None]
    if frames & (frames - 1):
        around = lax.all_gather(stats, "tm")
        count = 1 << (frames - 1).bit_length()
        order = reverse_bits(lax.iota(jnp.int32, count), count) ^ lax.axis_index("tm").astype(jnp.int32)
        return lax.psum(table, "tm"), jnp.take(around, jnp.minimum(order, frames - 1), axis=0)
    count = 1
    while count < frames:
        if count > 1:
            message = jnp.concatenate([gathered.reshape(-1, LANES), table])
        steps = [frames // (2 * count)]
        if 4 * count <= frames:
            steps += [frames // (4 * count), 3 * frames // (4 * count)]
        arrived = [lax.ppermute(message, "tm", [(i, i ^ step) for i in range(frames)]) for step in steps]
        table = table + sum(other[count * STAT_ROWS :] for other in arrived)
        gathered = jnp.concatenate([gathered] + [other[: count * STAT_ROWS].reshape(gathered.shape) for other in arrived])
        count *= len(steps) + 1
    return table, gathered


def on_device(queries, keys, values, d_out, action_table, actions, temporal_list):
    rows, width = queries.shape
    tiles = width // LANES
    frame = lax.axis_index("tm").astype(jnp.int32).reshape(1)
    wide = (rows, width)
    kv, qo = call(
        prepare_kernel,
        PREP,
        [((2 * rows + ACTION_ROWS, width), BF16, HOLD), ((2 * rows, width), BF16, HOLD)],
        [],
        [(array, False) for array in (actions.reshape(1, 1), keys, values, action_table, queries, d_out)],
    )
    near2, pair = shift(kv, 2), swap_pair(kv)
    late2, late_pair = shift(qo, -2), swap_pair(qo)
    partner, qo_partner = swap_row(kv), swap_row(qo)
    near3, near1 = shift(near2, 1), shift_some(pair, 2, 0)

    row_message, held, d_low, picked = call(
        forward_kernel,
        FWD,
        [
            ((STAT_ROWS + tiles * ACTIONS, LANES), F32, HOLD),
            (wide, BF16, HOLD),
            ((HEADS // 2, 2 * rows, 4 * rows), BF16, HOLD),
            ((2, 2 * rows + ACTION_ROWS, width), BF16, HOLD),
        ],
        [frame, temporal_list, actions],
        [(queries, False), (d_out, False)] + [(block, HOLD) for block in (kv, partner, near2, pair, near3, near1)],
    )
    attended, grad_queries = call(
        query_kernel,
        QUERY,
        [(wide, BF16, False), (wide, BF16, False)],
        [],
        [(block, HOLD) for block in (kv, partner, picked, d_low, held)],
    )
    late2, late_pair, _ = lax.optimization_barrier((late2, late_pair, held))
    late3 = shift(late2, -1)
    late1 = shift_some(late_pair, -2, 1)
    row_partner = swap_row(row_message[:STAT_ROWS])
    table, stats = share(row_message)
    table_partner = swap_row(table)
    near_keys, near_values = call(
        near_backward_kernel,
        NEAR,
        [(wide, F32, HOLD), (wide, F32, HOLD)],
        [],
        [(array, HOLD) for array in (kv, row_message, row_partner, qo, qo_partner)],
    )
    grad_keys, grad_values = call(
        far_backward_kernel,
        FAR,
        [(wide, BF16, False), (wide, BF16, False)],
        [frame],
        [(array, HOLD) for array in (kv, stats, near_keys, near_values, late2, late_pair, late3, late1)],
    )
    table_partner, grad_keys = lax.optimization_barrier((table_partner, grad_keys))
    table = table + table_partner
    grad_table = table.reshape(tiles, ACTIONS, LANES).transpose(1, 0, 2).reshape(ACTIONS, width)
    return attended, grad_queries, grad_keys, grad_values, grad_table


def solution(mesh):
    split = P(("grp", "tm", "row"), None)
    return jax.shard_map(
        on_device,
        mesh=mesh,
        in_specs=(split, split, split, split, P(), P(("grp", "tm")), split),
        out_specs=(split, split, split, split, P("grp", None)),
        check_vma=False,
    )
```

```python
import math

import jax
import jax.numpy as jnp
from jax import lax
from jax.experimental import pallas as pl
from jax.experimental.pallas import tpu as pltpu
from jax.sharding import PartitionSpec as P

HEADS = 8
HEAD_DIM = 96
LANES = 128
SCALE = 1.0 / math.sqrt(HEAD_DIM)
STAT_ROWS = 24
HOLD = True
PREP, FWD, NEAR, FAR, QUERY = 10**11, 10**10, 10**9, 10**9, 10**9
GROUP_ROWS = 16
ACTIONS = 8
EXP2_SCALE = SCALE * math.log2(math.e)
ACTION_ROWS = 8
MASKED = 1e30
F32 = jnp.float32
BF16 = jnp.bfloat16
VMEM_LIMIT = 56 * 1024 * 1024
SMALL_LIMIT = 12 * 1024 * 1024


def shift(block, distance):
    frames = range(lax.axis_size("tm"))
    return lax.ppermute(block, "tm", [(i - distance, i) for i in frames if i - distance in frames])


def shift_some(block, distance, parity):
    frames = range(lax.axis_size("tm"))
    route = [(i - distance, i) for i in frames if i - distance in frames and i % 2 == parity]
    return lax.ppermute(block, "tm", route)


def swap_pair(block):
    frames = range(lax.axis_size("tm"))
    return lax.ppermute(block, "tm", [(i, i ^ 1) for i in frames if i ^ 1 in frames])


def swap_row(block):
    return lax.ppermute(block, "row", [(0, 1), (1, 0)])


def pair_span(pair):
    first = 2 * pair * HEAD_DIM
    low = first // LANES * LANES
    high = -(-(first + 2 * HEAD_DIM) // LANES) * LANES
    return slice(low, high), (first - low, first - low + HEAD_DIM)


def split_pair(part, starts):
    lane = lax.broadcasted_iota(jnp.int32, part.shape, 1)
    none = jnp.zeros_like(part)
    return jnp.concatenate([jnp.where((lane >= start) & (lane < start + HEAD_DIM), part, none) for start in starts], axis=0)


def merge_pair(stacked, starts):
    half = stacked.shape[0] // 2
    lane = lax.broadcasted_iota(jnp.int32, (half, stacked.shape[1]), 1)
    return jnp.where(lane < starts[1], stacked[0:half], stacked[half:])


def join_pairs(parts):
    tiles = []
    for low in range(0, HEADS * HEAD_DIM, LANES):
        tile = None
        for pair in range(HEADS // 2):
            span, _ = pair_span(pair)
            if span.start <= low < span.stop:
                piece = parts[pair][:, low - span.start : low - span.start + LANES]
                if tile is None:
                    tile = piece
                else:
                    lane = lax.broadcasted_iota(jnp.int32, piece.shape, 1) + low
                    tile = jnp.where(lane >= 2 * pair * HEAD_DIM, piece, tile)
        tiles.append(tile)
    return tiles


def dot_t(left, right):
    return lax.dot_general(left, right, (((1,), (1,)), ((), ())), preferred_element_type=F32)


def dot(left, right):
    return jnp.dot(left, right, preferred_element_type=F32)


def prepare_kernel(actions, keys, values, table, queries, d_out, kv, qo):
    rows = values.shape[0]
    action = actions[...]
    label = lax.broadcasted_iota(jnp.int32, table.shape, 0)
    chosen = jnp.sum(jnp.where(label == action, table[...].astype(F32), 0.0), axis=0, keepdims=True)
    kv[0:rows, :] = keys[...]
    kv[rows : 2 * rows, :] = (values[...].astype(F32) + chosen).astype(BF16)
    kv[2 * rows :, :] = jnp.broadcast_to(action.astype(F32), (ACTION_ROWS, values.shape[1])).astype(BF16)
    qo[0:rows, :] = queries[...]
    qo[rows:, :] = d_out[...]


def forward_kernel(frame, listed, own_action, qo, own, partner, near2, pair, near3, near1,
                   row_message, attended, d_low, picked):
    rows = qo.shape[0] // 2
    frame_id = frame[0]
    odd = frame_id % 2
    present = []
    for slot in range(2):
        distance = listed[0, slot]
        code = jnp.where(distance == 1, jnp.where(odd == 1, 0, 1), distance)
        for value, source in ((0, pair), (1, near1), (2, near2), (3, near3)):
            @pl.when(code == value)
            def _(source=source, slot=slot):
                picked[slot] = source[...]
        present.append(frame_id >= distance)
    blocks = [own, partner, picked.at[0], picked.at[1]]
    lane = lax.broadcasted_iota(jnp.int32, (rows, LANES), 1)
    member_row = lax.broadcasted_iota(jnp.int32, (GROUP_ROWS, 4 * rows), 0)
    member_block = lax.broadcasted_iota(jnp.int32, (GROUP_ROWS, 4 * rows), 1) // rows
    members = jnp.where(jnp.maximum(member_block - 1, 0) == member_row, 1.0, 0.0).astype(BF16)
    columns = jnp.zeros((rows, LANES), F32)
    out_parts, sums = [], [[], [], []]
    for pair in range(HEADS // 2):
        span, starts = pair_span(pair)
        query = split_pair(qo[0:rows, span], starts)
        grad = split_pair(qo[rows:, span], starts)
        key = jnp.concatenate([block[0:rows, span] for block in blocks], axis=0)
        value = jnp.concatenate([block[rows : 2 * rows, span] for block in blocks], axis=0)
        scores = dot_t(query, key)
        scores = [scores[:, 0 : 2 * rows]] + [
            jnp.where(present[slot], scores[:, (2 + slot) * rows : (3 + slot) * rows], -MASKED) for slot in range(2)
        ]
        scores = jnp.concatenate(scores, axis=1)
        highest = jnp.max(scores, axis=1, keepdims=True)
        weights = jnp.exp2((scores - highest) * EXP2_SCALE)
        total = jnp.sum(weights, axis=1, keepdims=True)
        probs = weights * (1.0 / total)
        probs_low = probs.astype(BF16)
        out = dot(probs_low, value)
        d_probs = dot_t(grad, value)
        centre = jnp.sum(grad.astype(F32) * out, axis=1, keepdims=True)
        d_low[pair] = (probs * (d_probs - centre)).astype(BF16)
        out_parts.append(merge_pair(out, starts))
        log_total = highest * EXP2_SCALE + jnp.log2(total)
        for half in range(2):
            cut = slice(half * rows, (half + 1) * rows)
            columns = jnp.where(lane == 2 * pair + half, log_total[cut], columns)
            columns = jnp.where(lane == HEADS + 2 * pair + half, centre[cut], columns)
        mass = dot_t(members, probs_low)
        mass_high = mass.astype(BF16)
        mass_low = (mass - mass_high.astype(F32)).astype(BF16)
        weighted = dot(jnp.concatenate([mass_high, mass_low], axis=0), grad)
        weighted = weighted[0:GROUP_ROWS] + weighted[GROUP_ROWS:]
        for group in range(3):
            sums[group].append(weighted[group : group + 1])
    attended[...] = jnp.concatenate(join_pairs(out_parts), axis=1).astype(BF16)
    turned = columns.T
    row_message[0 : 2 * HEADS, :] = turned[0 : 2 * HEADS, :]
    which = lax.broadcasted_iota(jnp.int32, (HEADS, LANES), 0)
    in_list = (which == listed[0, 0]) | (which == listed[0, 1])
    row_message[2 * HEADS : STAT_ROWS, :] = jnp.where(in_list, 1.0, 0.0)
    tiles = [add_pairs(parts) for parts in sums]
    label = lax.broadcasted_iota(jnp.int32, (ACTIONS, LANES), 0).astype(F32)
    for index in range(len(tiles[0])):
        totals = jnp.zeros((ACTIONS, LANES), F32)
        cut = slice(index * LANES, (index + 1) * LANES)
        actions = [own_action[0].astype(F32)] + [picked[slot, 2 * rows :, cut].astype(F32)[0:1, :] for slot in range(2)]
        for group in range(3):
            action = actions[group]
            totals = totals + jnp.where(label == action, tiles[group][index], 0.0)
        row_message[STAT_ROWS + index * ACTIONS : STAT_ROWS + (index + 1) * ACTIONS, :] = totals


def query_kernel(own, partner, picked, d_low, held, arrived, attended, grad_queries):
    rows = held.shape[0]
    parts = []
    for pair in range(HEADS // 2):
        span, starts = pair_span(pair)
        key = jnp.concatenate([block[0:rows, span] for block in (own, partner, picked.at[0], picked.at[1])], axis=0)
        parts.append(merge_pair(dot(d_low[pair], key), starts))
    grad_queries[...] = (jnp.concatenate(join_pairs(parts), axis=1) * SCALE).astype(BF16)
    attended[...] = held[...]


def add_pairs(parts):
    tiles = []
    for low in range(0, HEADS * HEAD_DIM, LANES):
        tile = None
        for pair in range(HEADS // 2):
            span, _ = pair_span(pair)
            if span.start <= low < span.stop:
                piece = parts[pair][:, low - span.start : low - span.start + LANES]
                tile = piece if tile is None else tile + piece
        tiles.append(tile)
    return tiles


def backward_pairs(own, sources, log_totals, centres):
    rows = (own.shape[0] - ACTION_ROWS) // 2
    key_parts, value_parts = [], []
    for pair in range(HEADS // 2):
        span, starts = pair_span(pair)
        key = split_pair(own[0:rows, span], starts)
        value = split_pair(own[rows : 2 * rows, span], starts)
        query = jnp.concatenate([source(slice(0, rows), span) for source in sources], axis=0)
        grad = jnp.concatenate([source(slice(rows, 2 * rows), span) for source in sources], axis=0)
        scores = dot_t(key, query)
        d_probs = dot_t(value, grad)
        low, d_low = [], []
        for half in range(2):
            head = 2 * pair + half
            cut = slice(half * rows, (half + 1) * rows)
            probs = jnp.exp2(scores[cut] * EXP2_SCALE - log_totals[head : head + 1, :])
            low.append(probs.astype(BF16))
            d_low.append((probs * (d_probs[cut] - centres[head : head + 1, :])).astype(BF16))
        value_parts.append(merge_pair(dot(jnp.concatenate(low, axis=0), grad), starts))
        key_parts.append(merge_pair(dot(jnp.concatenate(d_low, axis=0), query), starts))
    return jnp.concatenate(join_pairs(key_parts), axis=1), jnp.concatenate(join_pairs(value_parts), axis=1)


def reader(ref):
    return lambda rows, lanes: ref[rows, lanes]


def near_backward_kernel(own, row_own, row_partner, qo, qo_partner, near_keys, near_values):
    log_totals = jnp.concatenate([row_own[0:HEADS, :], row_partner[0:HEADS, :]], axis=1)
    centres = jnp.concatenate([row_own[HEADS : 2 * HEADS, :], row_partner[HEADS : 2 * HEADS, :]], axis=1)
    sources = [reader(qo), reader(qo_partner)]
    near_keys[...], near_values[...] = backward_pairs(own, sources, log_totals, centres)


def reverse_bits(index, count):
    bits = (count - 1).bit_length()
    return sum(((index >> bit) & 1) << (bits - 1 - bit) for bit in range(bits))


def far_backward_kernel(frame, own, stats, near_keys, near_values, late2, late_pair, late3, late1,
                        grad_keys, grad_values):
    frame_id = frame[0]
    odd = frame_id % 2 == 1
    sources = [lambda rows, lanes: jnp.where(odd, late1[rows, lanes], late_pair[rows, lanes]), reader(late2), reader(late3)]
    log_totals, centres = [], []
    for distance in (1, 2, 3):
        later = frame_id + distance
        exists = later < stats.shape[0]
        block = stats[jnp.where(exists, reverse_bits(later ^ frame_id, stats.shape[0]), 0)]
        uses = exists & (block[2 * HEADS + distance : 2 * HEADS + distance + 1, :] > 0.5)
        log_totals.append(jnp.where(uses, block[0:HEADS, :], MASKED))
        centres.append(block[HEADS : 2 * HEADS, :])
    log_totals = jnp.concatenate(log_totals, axis=1)
    centres = jnp.concatenate(centres, axis=1)
    far_keys, far_values = backward_pairs(own, sources, log_totals, centres)
    grad_keys[...] = ((near_keys[...] + far_keys) * SCALE).astype(BF16)
    grad_values[...] = (near_values[...] + far_values).astype(BF16)


VMEM, SMEM = pltpu.VMEM, pltpu.SMEM


def call(kernel, flops, outs, scalars, arrays, scratch=()):
    return pl.pallas_call(
        kernel,
        out_shape=tuple(pltpu.VMEM(shape, dtype) if stays else jax.ShapeDtypeStruct(shape, dtype) for shape, dtype, stays in outs),
        in_specs=[pl.BlockSpec(memory_space=SMEM)] * len(scalars) + [pl.BlockSpec(memory_space=VMEM)] * len(arrays),
        out_specs=(pl.BlockSpec(memory_space=VMEM),) * len(outs),
        scratch_shapes=list(scratch),
        compiler_params=pltpu.CompilerParams(vmem_limit_bytes=VMEM_LIMIT if flops in (PREP, FWD) else SMALL_LIMIT),
        cost_estimate=pl.CostEstimate(flops=flops, transcendentals=0, bytes_accessed=0),
    )(*scalars, *[pltpu.with_memory_space_constraint(array, VMEM) if hold else array for array, hold in arrays])


def share(message):
    frames = lax.axis_size("tm")
    stats, table = message[:STAT_ROWS], message[STAT_ROWS:]
    gathered = stats[None]
    if frames & (frames - 1):
        around = lax.all_gather(stats, "tm")
        count = 1 << (frames - 1).bit_length()
        order = reverse_bits(lax.iota(jnp.int32, count), count) ^ lax.axis_index("tm").astype(jnp.int32)
        return lax.psum(table, "tm"), jnp.take(around, jnp.minimum(order, frames - 1), axis=0), message
    count = 1
    while count < frames:
        if count > 1:
            message = jnp.concatenate([gathered.reshape(-1, LANES), table])
        steps = [frames // (2 * count)]
        if 4 * count <= frames:
            steps += [frames // (4 * count), 3 * frames // (4 * count)]
        arrived = [lax.ppermute(message, "tm", [(i, i ^ step) for i in range(frames)]) for step in steps]
        table = table + sum(other[count * STAT_ROWS :] for other in arrived)
        gathered = jnp.concatenate([gathered] + [other[: count * STAT_ROWS].reshape(gathered.shape) for other in arrived])
        if count == 1:
            first = arrived[0]
        count *= len(steps) + 1
    return table, gathered, first


def on_device(queries, keys, values, d_out, action_table, actions, temporal_list):
    rows, width = queries.shape
    tiles = width // LANES
    frame = lax.axis_index("tm").astype(jnp.int32).reshape(1)
    wide = (rows, width)
    kv, qo = call(
        prepare_kernel,
        PREP,
        [((2 * rows + ACTION_ROWS, width), BF16, HOLD), ((2 * rows, width), BF16, HOLD)],
        [],
        [(array, False) for array in (actions.reshape(1, 1), keys, values, action_table, queries, d_out)],
    )
    near2, pair = shift(kv, 2), swap_pair(kv)
    late2, late_pair = shift(qo, -2), swap_pair(qo)
    partner, qo_partner = swap_row(kv), swap_row(qo)
    near3, near1 = shift(near2, 1), shift_some(pair, 2, 0)

    row_message, held, d_low, picked = call(
        forward_kernel,
        FWD,
        [
            ((STAT_ROWS + tiles * ACTIONS, LANES), F32, HOLD),
            (wide, BF16, HOLD),
            ((HEADS // 2, 2 * rows, 4 * rows), BF16, HOLD),
            ((2, 2 * rows + ACTION_ROWS, width), BF16, HOLD),
        ],
        [frame, temporal_list, actions],
        [(block, HOLD) for block in (qo, kv, partner, near2, pair, near3, near1)],
    )
    late2, late_pair, _ = lax.optimization_barrier((late2, late_pair, held))
    late3 = shift(late2, -1)
    late1 = shift_some(late_pair, -2, 1)
    row_partner = swap_row(row_message[:STAT_ROWS])
    table, stats, first = share(row_message)
    table_partner = swap_row(table)
    attended, grad_queries = call(
        query_kernel,
        QUERY,
        [(wide, BF16, False), (wide, BF16, False)],
        [],
        [(block, HOLD) for block in (kv, partner, picked, d_low, held, first)],
    )
    near_keys, near_values = call(
        near_backward_kernel,
        NEAR,
        [(wide, F32, HOLD), (wide, F32, HOLD)],
        [],
        [(array, HOLD) for array in (kv, row_message, row_partner, qo, qo_partner)],
    )
    grad_keys, grad_values = call(
        far_backward_kernel,
        FAR,
        [(wide, BF16, False), (wide, BF16, False)],
        [frame],
        [(array, HOLD) for array in (kv, stats, near_keys, near_values, late2, late_pair, late3, late1)],
    )
    table_partner, grad_keys = lax.optimization_barrier((table_partner, grad_keys))
    table = table + table_partner
    grad_table = table.reshape(tiles, ACTIONS, LANES).transpose(1, 0, 2).reshape(ACTIONS, width)
    return attended, grad_queries, grad_keys, grad_values, grad_table


def solution(mesh):
    split = P(("grp", "tm", "row"), None)
    return jax.shard_map(
        on_device,
        mesh=mesh,
        in_specs=(split, split, split, split, P(), P(("grp", "tm")), split),
        out_specs=(split, split, split, split, P("grp", None)),
        check_vma=False,
    )
```

```python
import math

import jax
import jax.numpy as jnp
from jax import lax
from jax.experimental import pallas as pl
from jax.experimental.pallas import tpu as pltpu
from jax.sharding import PartitionSpec as P

HEADS = 8
HEAD_DIM = 96
LANES = 128
SCALE = 1.0 / math.sqrt(HEAD_DIM)
STAT_ROWS = 24
HOLD = True
PREP, FWD, NEAR, FAR, QUERY = 10**11, 10**10, 10**9, 10**9, 10**9
GROUP_ROWS = 16
ACTIONS = 8
EXP2_SCALE = SCALE * math.log2(math.e)
ACTION_ROWS = 8
MASKED = 1e30
F32 = jnp.float32
BF16 = jnp.bfloat16
VMEM_LIMIT = 56 * 1024 * 1024
SMALL_LIMIT = 12 * 1024 * 1024


def shift(block, distance):
    frames = range(lax.axis_size("tm"))
    return lax.ppermute(block, "tm", [(i - distance, i) for i in frames if i - distance in frames])


def shift_some(block, distance, parity):
    frames = range(lax.axis_size("tm"))
    route = [(i - distance, i) for i in frames if i - distance in frames and i % 2 == parity]
    return lax.ppermute(block, "tm", route)


def swap_pair(block):
    frames = range(lax.axis_size("tm"))
    return lax.ppermute(block, "tm", [(i, i ^ 1) for i in frames if i ^ 1 in frames])


def swap_row(block):
    return lax.ppermute(block, "row", [(0, 1), (1, 0)])


def pair_span(pair):
    first = 2 * pair * HEAD_DIM
    low = first // LANES * LANES
    high = -(-(first + 2 * HEAD_DIM) // LANES) * LANES
    return slice(low, high), (first - low, first - low + HEAD_DIM)


def split_pair(part, starts):
    lane = lax.broadcasted_iota(jnp.int32, part.shape, 1)
    none = jnp.zeros_like(part)
    return jnp.concatenate([jnp.where((lane >= start) & (lane < start + HEAD_DIM), part, none) for start in starts], axis=0)


def merge_pair(stacked, starts):
    half = stacked.shape[0] // 2
    lane = lax.broadcasted_iota(jnp.int32, (half, stacked.shape[1]), 1)
    return jnp.where(lane < starts[1], stacked[0:half], stacked[half:])


def join_pairs(parts):
    tiles = []
    for low in range(0, HEADS * HEAD_DIM, LANES):
        tile = None
        for pair in range(HEADS // 2):
            span, _ = pair_span(pair)
            if span.start <= low < span.stop:
                piece = parts[pair][:, low - span.start : low - span.start + LANES]
                if tile is None:
                    tile = piece
                else:
                    lane = lax.broadcasted_iota(jnp.int32, piece.shape, 1) + low
                    tile = jnp.where(lane >= 2 * pair * HEAD_DIM, piece, tile)
        tiles.append(tile)
    return tiles


def dot_t(left, right):
    return lax.dot_general(left, right, (((1,), (1,)), ((), ())), preferred_element_type=F32)


def dot(left, right):
    return jnp.dot(left, right, preferred_element_type=F32)


def prepare_kernel(actions, keys, values, table, queries, d_out, kv, qo):
    rows = values.shape[0]
    action = actions[...]
    label = lax.broadcasted_iota(jnp.int32, table.shape, 0)
    chosen = jnp.sum(jnp.where(label == action, table[...].astype(F32), 0.0), axis=0, keepdims=True)
    kv[0:rows, :] = keys[...]
    kv[rows : 2 * rows, :] = (values[...].astype(F32) + chosen).astype(BF16)
    kv[2 * rows :, :] = jnp.broadcast_to(action.astype(F32), (ACTION_ROWS, values.shape[1])).astype(BF16)
    qo[0:rows, :] = queries[...]
    qo[rows:, :] = d_out[...]


def forward_kernel(frame, listed, own_action, qo, own, partner, near2, pair, near3, near1,
                   row_message, attended, d_low, picked):
    rows = qo.shape[0] // 2
    frame_id = frame[0]
    odd = frame_id % 2
    present = []
    for slot in range(2):
        distance = listed[0, slot]
        code = jnp.where(distance == 1, jnp.where(odd == 1, 0, 1), distance)
        for value, source in ((0, pair), (1, near1), (2, near2), (3, near3)):
            @pl.when(code == value)
            def _(source=source, slot=slot):
                picked[slot] = source[...]
        present.append(frame_id >= distance)
    blocks = [own, partner, picked.at[0], picked.at[1]]
    lane = lax.broadcasted_iota(jnp.int32, (rows, LANES), 1)
    member_row = lax.broadcasted_iota(jnp.int32, (GROUP_ROWS, 4 * rows), 0)
    member_block = lax.broadcasted_iota(jnp.int32, (GROUP_ROWS, 4 * rows), 1) // rows
    members = jnp.where(jnp.maximum(member_block - 1, 0) == member_row, 1.0, 0.0).astype(BF16)
    columns = jnp.zeros((rows, LANES), F32)
    out_parts, sums = [], [[], [], []]
    for pair in range(HEADS // 2):
        span, starts = pair_span(pair)
        query = split_pair(qo[0:rows, span], starts)
        grad = split_pair(qo[rows:, span], starts)
        key = jnp.concatenate([block[0:rows, span] for block in blocks], axis=0)
        value = jnp.concatenate([block[rows : 2 * rows, span] for block in blocks], axis=0)
        scores = dot_t(query, key)
        scores = [scores[:, 0 : 2 * rows]] + [
            jnp.where(present[slot], scores[:, (2 + slot) * rows : (3 + slot) * rows], -MASKED) for slot in range(2)
        ]
        scores = jnp.concatenate(scores, axis=1)
        highest = jnp.max(scores, axis=1, keepdims=True)
        weights = jnp.exp2((scores - highest) * EXP2_SCALE)
        total = jnp.sum(weights, axis=1, keepdims=True)
        probs = weights * (1.0 / total)
        probs_low = probs.astype(BF16)
        out = dot(probs_low, value)
        d_probs = dot_t(grad, value)
        centre = jnp.sum(grad.astype(F32) * out, axis=1, keepdims=True)
        d_low[pair] = (probs * (d_probs - centre)).astype(BF16)
        out_parts.append(merge_pair(out, starts))
        log_total = highest * EXP2_SCALE + jnp.log2(total)
        for half in range(2):
            cut = slice(half * rows, (half + 1) * rows)
            columns = jnp.where(lane == 2 * pair + half, log_total[cut], columns)
            columns = jnp.where(lane == HEADS + 2 * pair + half, centre[cut], columns)
        mass = dot_t(members, probs_low)
        mass_high = mass.astype(BF16)
        mass_low = (mass - mass_high.astype(F32)).astype(BF16)
        weighted = dot(jnp.concatenate([mass_high, mass_low], axis=0), grad)
        weighted = weighted[0:GROUP_ROWS] + weighted[GROUP_ROWS:]
        for group in range(3):
            sums[group].append(weighted[group : group + 1])
    attended[...] = jnp.concatenate(join_pairs(out_parts), axis=1).astype(BF16)
    turned = columns.T
    row_message[0 : 2 * HEADS, :] = turned[0 : 2 * HEADS, :]
    which = lax.broadcasted_iota(jnp.int32, (HEADS, LANES), 0)
    in_list = (which == listed[0, 0]) | (which == listed[0, 1])
    row_message[2 * HEADS : STAT_ROWS, :] = jnp.where(in_list, 1.0, 0.0)
    tiles = [add_pairs(parts) for parts in sums]
    label = lax.broadcasted_iota(jnp.int32, (ACTIONS, LANES), 0).astype(F32)
    for index in range(len(tiles[0])):
        totals = jnp.zeros((ACTIONS, LANES), F32)
        cut = slice(index * LANES, (index + 1) * LANES)
        actions = [own_action[0].astype(F32)] + [picked[slot, 2 * rows :, cut].astype(F32)[0:1, :] for slot in range(2)]
        for group in range(3):
            action = actions[group]
            totals = totals + jnp.where(label == action, tiles[group][index], 0.0)
        row_message[STAT_ROWS + index * ACTIONS : STAT_ROWS + (index + 1) * ACTIONS, :] = totals


def query_kernel(own, partner, picked, d_low, held, arrived, attended, grad_queries):
    rows = held.shape[0]
    parts = []
    for pair in range(HEADS // 2):
        span, starts = pair_span(pair)
        key = jnp.concatenate([block[0:rows, span] for block in (own, partner, picked.at[0], picked.at[1])], axis=0)
        parts.append(merge_pair(dot(d_low[pair], key), starts))
    grad_queries[...] = (jnp.concatenate(join_pairs(parts), axis=1) * SCALE).astype(BF16)
    attended[...] = held[...]


def add_pairs(parts):
    tiles = []
    for low in range(0, HEADS * HEAD_DIM, LANES):
        tile = None
        for pair in range(HEADS // 2):
            span, _ = pair_span(pair)
            if span.start <= low < span.stop:
                piece = parts[pair][:, low - span.start : low - span.start + LANES]
                tile = piece if tile is None else tile + piece
        tiles.append(tile)
    return tiles


def backward_pairs(own, sources, log_totals, centres):
    rows = (own.shape[0] - ACTION_ROWS) // 2
    key_parts, value_parts = [], []
    for pair in range(HEADS // 2):
        span, starts = pair_span(pair)
        key = split_pair(own[0:rows, span], starts)
        value = split_pair(own[rows : 2 * rows, span], starts)
        query = jnp.concatenate([source(slice(0, rows), span) for source in sources], axis=0)
        grad = jnp.concatenate([source(slice(rows, 2 * rows), span) for source in sources], axis=0)
        scores = dot_t(key, query)
        d_probs = dot_t(value, grad)
        low, d_low = [], []
        for half in range(2):
            head = 2 * pair + half
            cut = slice(half * rows, (half + 1) * rows)
            probs = jnp.exp2(scores[cut] * EXP2_SCALE - log_totals[head : head + 1, :])
            low.append(probs.astype(BF16))
            d_low.append((probs * (d_probs[cut] - centres[head : head + 1, :])).astype(BF16))
        value_parts.append(merge_pair(dot(jnp.concatenate(low, axis=0), grad), starts))
        key_parts.append(merge_pair(dot(jnp.concatenate(d_low, axis=0), query), starts))
    return jnp.concatenate(join_pairs(key_parts), axis=1), jnp.concatenate(join_pairs(value_parts), axis=1)


def reader(ref):
    return lambda rows, lanes: ref[rows, lanes]


def near_backward_kernel(own, row_own, row_partner, qo, qo_partner, near_keys, near_values):
    log_totals = jnp.concatenate([row_own[0:HEADS, :], row_partner[0:HEADS, :]], axis=1)
    centres = jnp.concatenate([row_own[HEADS : 2 * HEADS, :], row_partner[HEADS : 2 * HEADS, :]], axis=1)
    sources = [reader(qo), reader(qo_partner)]
    near_keys[...], near_values[...] = backward_pairs(own, sources, log_totals, centres)


def reverse_bits(index, count):
    bits = (count - 1).bit_length()
    return sum(((index >> bit) & 1) << (bits - 1 - bit) for bit in range(bits))


def far_backward_kernel(frame, own, stats, near_keys, near_values, late2, late_pair, late3, late1,
                        grad_keys, grad_values):
    frame_id = frame[0]
    odd = frame_id % 2 == 1
    sources = [lambda rows, lanes: jnp.where(odd, late1[rows, lanes], late_pair[rows, lanes]), reader(late2), reader(late3)]
    log_totals, centres = [], []
    for distance in (1, 2, 3):
        later = frame_id + distance
        exists = later < stats.shape[0]
        block = stats[jnp.where(exists, reverse_bits(later ^ frame_id, stats.shape[0]), 0)]
        uses = exists & (block[2 * HEADS + distance : 2 * HEADS + distance + 1, :] > 0.5)
        log_totals.append(jnp.where(uses, block[0:HEADS, :], MASKED))
        centres.append(block[HEADS : 2 * HEADS, :])
    log_totals = jnp.concatenate(log_totals, axis=1)
    centres = jnp.concatenate(centres, axis=1)
    far_keys, far_values = backward_pairs(own, sources, log_totals, centres)
    grad_keys[...] = ((near_keys[...] + far_keys) * SCALE).astype(BF16)
    grad_values[...] = (near_values[...] + far_values).astype(BF16)


VMEM, SMEM = pltpu.VMEM, pltpu.SMEM


def call(kernel, flops, outs, scalars, arrays, scratch=()):
    return pl.pallas_call(
        kernel,
        out_shape=tuple(pltpu.VMEM(shape, dtype) if stays else jax.ShapeDtypeStruct(shape, dtype) for shape, dtype, stays in outs),
        in_specs=[pl.BlockSpec(memory_space=SMEM)] * len(scalars) + [pl.BlockSpec(memory_space=VMEM)] * len(arrays),
        out_specs=(pl.BlockSpec(memory_space=VMEM),) * len(outs),
        scratch_shapes=list(scratch),
        compiler_params=pltpu.CompilerParams(vmem_limit_bytes=VMEM_LIMIT if flops == PREP else SMALL_LIMIT),
        cost_estimate=pl.CostEstimate(flops=flops, transcendentals=0, bytes_accessed=0),
    )(*scalars, *[pltpu.with_memory_space_constraint(array, VMEM) if hold else array for array, hold in arrays])


def share(message):
    frames = lax.axis_size("tm")
    stats, table = message[:STAT_ROWS], message[STAT_ROWS:]
    gathered = stats[None]
    if frames & (frames - 1):
        around = lax.all_gather(stats, "tm")
        count = 1 << (frames - 1).bit_length()
        order = reverse_bits(lax.iota(jnp.int32, count), count) ^ lax.axis_index("tm").astype(jnp.int32)
        return lax.psum(table, "tm"), jnp.take(around, jnp.minimum(order, frames - 1), axis=0), message
    count = 1
    while count < frames:
        if count > 1:
            message = jnp.concatenate([gathered.reshape(-1, LANES), table])
        steps = [frames // (2 * count)]
        if 4 * count <= frames:
            steps += [frames // (4 * count), 3 * frames // (4 * count)]
        arrived = [lax.ppermute(message, "tm", [(i, i ^ step) for i in range(frames)]) for step in steps]
        table = table + sum(other[count * STAT_ROWS :] for other in arrived)
        gathered = jnp.concatenate([gathered] + [other[: count * STAT_ROWS].reshape(gathered.shape) for other in arrived])
        if count == 1:
            first = arrived[0]
        count *= len(steps) + 1
    return table, gathered, first


def on_device(queries, keys, values, d_out, action_table, actions, temporal_list):
    rows, width = queries.shape
    tiles = width // LANES
    frame = lax.axis_index("tm").astype(jnp.int32).reshape(1)
    wide = (rows, width)
    kv, qo = call(
        prepare_kernel,
        PREP,
        [((2 * rows + ACTION_ROWS, width), BF16, HOLD), ((2 * rows, width), BF16, HOLD)],
        [],
        [(array, False) for array in (actions.reshape(1, 1), keys, values, action_table, queries, d_out)],
    )
    near2, pair = shift(kv, 2), swap_pair(kv)
    late2, late_pair = shift(qo, -2), swap_pair(qo)
    partner, qo_partner = swap_row(kv), swap_row(qo)
    near3, near1 = shift(near2, 1), shift_some(pair, 2, 0)

    row_message, held, d_low, picked = call(
        forward_kernel,
        FWD,
        [
            ((STAT_ROWS + tiles * ACTIONS, LANES), F32, HOLD),
            (wide, BF16, HOLD),
            ((HEADS // 2, 2 * rows, 4 * rows), BF16, HOLD),
            ((2, 2 * rows + ACTION_ROWS, width), BF16, HOLD),
        ],
        [frame, temporal_list, actions],
        [(block, HOLD) for block in (qo, kv, partner, near2, pair, near3, near1)],
    )
    late2, late_pair, _ = lax.optimization_barrier((late2, late_pair, held))
    late3 = shift(late2, -1)
    late1 = shift_some(late_pair, -2, 1)
    row_partner = swap_row(row_message[:STAT_ROWS])
    table, stats, first = share(row_message)
    table_partner = swap_row(table)
    attended, grad_queries = call(
        query_kernel,
        QUERY,
        [(wide, BF16, False), (wide, BF16, False)],
        [],
        [(block, HOLD) for block in (kv, partner, picked, d_low, held, first)],
    )
    near_keys, near_values = call(
        near_backward_kernel,
        NEAR,
        [(wide, F32, HOLD), (wide, F32, HOLD)],
        [],
        [(array, HOLD) for array in (kv, row_message, row_partner, qo, qo_partner)],
    )
    grad_keys, grad_values = call(
        far_backward_kernel,
        FAR,
        [(wide, BF16, False), (wide, BF16, False)],
        [frame],
        [(array, HOLD) for array in (kv, stats, near_keys, near_values, late2, late_pair, late3, late1)],
    )
    table_partner, grad_keys = lax.optimization_barrier((table_partner, grad_keys))
    table = table + table_partner
    grad_table = table.reshape(tiles, ACTIONS, LANES).transpose(1, 0, 2).reshape(ACTIONS, width)
    return attended, grad_queries, grad_keys, grad_values, grad_table


def solution(mesh):
    split = P(("grp", "tm", "row"), None)
    return jax.shard_map(
        on_device,
        mesh=mesh,
        in_specs=(split, split, split, split, P(), P(("grp", "tm")), split),
        out_specs=(split, split, split, split, P("grp", None)),
        check_vma=False,
    )
```
